128 devices in a mesh: grp: 4 (over x), dev: 32 (over y, z, core).
Axes of the slice: x: 4, y: 4, z: 4, core: 2. Of those that a mesh axis runs over, the one named last changes fastest.
Arguments:
- queries: bfloat16 [32768, 4096], P(('grp', 'dev')), may hold values from -500 to 500
- new_kv: bfloat16 [32768, 2048], P(('grp', 'dev')), may hold values from -6 to 6
- kv_pool: bfloat16 [8192, 16, 2048], P(('grp', 'dev')), may hold values from -6 to 6
- hit_holder: int32 [128, 96], P(('grp', 'dev')), may hold values from 0 to 127, as said below
- hit_block: int32 [128, 96], P(('grp', 'dev')), may hold values from 0 to 63
- hit_count: int32 [128], P(('grp', 'dev')), may hold values from 48 to 96
- ssm_input: bfloat16 [32768, 8192], P(('grp', 'dev')), may hold values from -6 to 6
- step_size: float32 [32768, 128], P(('grp', 'dev')), may hold values from 0.04 to 0.16
- decay_rate: float32 [128], replicated, may hold values from 0.01 to 0.4
- state_in: float32 [32768, 16], P(('grp', 'dev')), may hold values from -6 to 6
- state_out: float32 [32768, 16], P(('grp', 'dev')), may hold values from -6 to 6
- skip_gain: float32 [128], replicated, may hold values from 0.1 to 1.9
- state_pool: float32 [256, 16, 8192], P(('grp', 'dev')), may hold values from -3 to 3
- state_group: int32 [128], P(('grp', 'dev')), may hold values from 0 to 3
- state_slot: int32 [128], P(('grp', 'dev')), may hold values from 0 to 1
Outputs:
- attended: bfloat16 [32768, 4096], P(('grp', 'dev'))
- mixed: bfloat16 [32768, 8192], P(('grp', 'dev'))
The draws below stay inside these ranges and needn't reach their ends.
Inputs may be any that keep to these rules, and one draw needn't show every extreme that they name: `hit_holder`: the first hit_count entries of a row name different holder devices.
All inputs are finite; a program needn't handle non-finite values.
Results may differ from the reference program's by a relative error of at most 0.0027.
Values may be sent and summed in bfloat16 or wider, within the bound.
A program may use at most 256 MiB of HBM per device.

```python
import jax
import jax.numpy as jnp
from jax import lax

D = 4096
HEADS = 32
KV_HEADS = 8
HEAD_DIM = 128
DI = 8192
NS = 16
SSM_HEAD_DIM = 64
SSM_HEADS = 128
KVW = 2048
SUF = 256
BLK = 16
POOL = 64
SLOTS = 2
HIT_MAX = 96
TOKENS = 32768
N_GRP = 4
N_DEV = 32
DEVICES = 128


def draw_queries(key, part):
    base = jax.random.normal(key, (TOKENS, D), jnp.float32) * 3.0
    return jnp.clip(base, -500.0, 500.0).astype(jnp.bfloat16)


def draw_decay_rate(key, part):
    unit = jax.random.uniform(key, (SSM_HEADS,), jnp.float32)
    return jnp.exp(jnp.log(0.01) + unit * (jnp.log(0.4) - jnp.log(0.01)))


def draw_hit_holder(key, part):
    keys = jax.random.split(key, DEVICES)
    return jax.vmap(lambda k: jax.random.permutation(k, DEVICES)[:HIT_MAX])(keys).astype(jnp.int32)


def draw_hit_count(key, part):
    counts = jax.random.randint(key, (DEVICES,), HIT_MAX // 2, HIT_MAX + 1, jnp.int32)
    fullest = jax.random.randint(jax.random.fold_in(key, 1), (), 0, DEVICES, jnp.int32)
    return counts.at[fullest].set(HIT_MAX)


def set_ends(values, key, low, largest):
    longest = values.shape.index(max(values.shape))
    spots = []
    for shift in (0, 1):
        where = [jax.random.randint(jax.random.fold_in(key, axis), (), 0, length) for axis, length in enumerate(values.shape)]
        where[longest] = (where[longest] + shift) % values.shape[longest]
        spots.append(tuple(where))
    return values.at[spots[0]].set(low).at[spots[1]].set(largest)


def block_scale(own_key, extent, cuts, smallest, largest):
    def one(position, shards_of):
        heights = jax.random.uniform(jax.random.fold_in(jax.random.fold_in(own_key, 6), position), (shards_of,), jnp.float32, smallest / len(cuts), largest / len(cuts))
        return jnp.repeat(jnp.exp(heights), extent[position] // shards_of).reshape((-1,) + (1,) * (len(extent) - position - 1))

    factor_of = one(*cuts[0])
    for cut in cuts[1:]:
        factor_of = factor_of * one(*cut)
    return factor_of


def centred(stream_key, extent, deviation, limit, shards=(), kind=jnp.bfloat16):
    drawn = jax.random.normal(stream_key, extent, jnp.float32) * deviation
    if len(shards) > 0:
        drawn = block_scale(stream_key, extent, shards, -0.22, 0.18) * drawn
    return jnp.clip(drawn, min=-limit, max=limit).astype(kind)


def setup_inputs(seed: int = 0) -> dict:
    arg_keys = jax.random.split(jax.random.key(seed), 16)
    return {
        "queries": draw_queries(jax.random.fold_in(arg_keys[15], 71), 0),
        "new_kv": centred(arg_keys[1], (TOKENS, KVW), 1.0, 6.0, ((0, 128),)),
        "kv_pool": centred(arg_keys[2], (DEVICES * POOL, BLK, KVW), 1.0, 6.0, ((0, 128),)),
        "hit_holder": draw_hit_holder(jax.random.fold_in(arg_keys[15], 71), 0),
        "hit_block": set_ends(jax.random.randint(arg_keys[4], (DEVICES, HIT_MAX), 0, POOL), jax.random.fold_in(arg_keys[4], 1), 0, POOL - 1).astype(jnp.int32),
        "hit_count": draw_hit_count(jax.random.fold_in(arg_keys[15], 71), 0),
        "ssm_input": centred(arg_keys[6], (TOKENS, DI), 1.0, 6.0, ((0, 128),)),
        "step_size": jnp.clip(0.04 + 0.12 * jax.random.uniform(arg_keys[7], (TOKENS, SSM_HEADS), jnp.float32) ** block_scale(arg_keys[7], (TOKENS, SSM_HEADS), ((0, 128),), -0.2, 0.2), 0.04, 0.16),
        "decay_rate": draw_decay_rate(jax.random.fold_in(arg_keys[15], 71), 0),
        "state_in": centred(arg_keys[9], (TOKENS, NS), 1.0, 6.0, ((0, 128),), jnp.float32),
        "state_out": centred(arg_keys[10], (TOKENS, NS), 1.0, 6.0, ((0, 128),), jnp.float32),
        "skip_gain": jnp.clip(1.0 + 0.18 * jax.random.normal(arg_keys[11], (SSM_HEADS,), jnp.float32), 0.1, 1.9),
        "state_pool": centred(arg_keys[12], (DEVICES * SLOTS, NS, DI), 0.5, 3.0, ((0, 128),), jnp.float32),
        "state_group": set_ends(jax.random.randint(arg_keys[13], (DEVICES,), 0, N_GRP), jax.random.fold_in(arg_keys[13], 1), 0, N_GRP - 1).astype(jnp.int32),
        "state_slot": set_ends(jax.random.randint(arg_keys[14], (DEVICES,), 0, SLOTS), jax.random.fold_in(arg_keys[14], 1), 0, SLOTS - 1).astype(jnp.int32),
    }


def attend_one(qrows, keys_all, allowed):
    group = HEADS // KV_HEADS
    length = keys_all.shape[0]
    qh = qrows.reshape(SUF, KV_HEADS, group, HEAD_DIM).astype(jnp.float32)
    keys = keys_all[:, :KV_HEADS * HEAD_DIM].reshape(length, KV_HEADS, HEAD_DIM).astype(jnp.float32)
    values = keys_all[:, KV_HEADS * HEAD_DIM:].reshape(length, KV_HEADS, HEAD_DIM).astype(jnp.float32)
    scores = jnp.einsum("qhgd,khd->hgqk", qh, keys) * (HEAD_DIM ** -0.5)
    scores = jnp.where(allowed[None, None], scores, -1e30)
    top = jnp.max(scores, axis=-1, keepdims=True)
    weights = jnp.exp(scores - top)
    total = jnp.sum(weights, axis=-1)
    rounded = weights.astype(jnp.bfloat16).astype(jnp.float32)
    numer = jnp.einsum("hgqk,khd->qhgd", rounded, values)
    result = numer / jnp.transpose(total, (2, 0, 1))[:, :, :, None]
    return result.reshape(SUF, HEADS * HEAD_DIM).astype(jnp.bfloat16)


def reference(queries, new_kv, kv_pool, hit_holder, hit_block, hit_count, ssm_input, step_size, decay_rate, state_in, state_out, skip_gain, state_pool, state_group, state_slot):
    entries = jnp.arange(HIT_MAX, dtype=jnp.int32)
    positions = jnp.arange(SUF, dtype=jnp.int32)
    causal = positions[None, :] <= positions[:, None]

    def per_request(index):
        start = (index * SUF).astype(jnp.int32)
        qrows = lax.dynamic_slice_in_dim(queries, start, SUF, 0)
        own = lax.dynamic_slice_in_dim(new_kv, start, SUF, 0)
        rows = hit_holder[index] * POOL + hit_block[index]
        prefix = kv_pool[rows].reshape(HIT_MAX * BLK, KVW)
        live = jnp.repeat(entries < hit_count[index], BLK)
        keys_all = jnp.concatenate([prefix, own], axis=0)
        allowed = jnp.concatenate([jnp.broadcast_to(live[None, :], (SUF, HIT_MAX * BLK)), causal], axis=1)
        return attend_one(qrows, keys_all, allowed)

    attended = lax.map(per_request, jnp.arange(DEVICES, dtype=jnp.int32)).reshape(TOKENS, D)

    requester = jnp.arange(DEVICES, dtype=jnp.int32)
    where_state = (state_group * N_DEV + requester % N_DEV) * SLOTS + state_slot
    state = state_pool[where_state].reshape(DEVICES, NS, SSM_HEADS, SSM_HEAD_DIM)
    inputs = ssm_input.astype(jnp.float32).reshape(DEVICES, SUF, SSM_HEADS, SSM_HEAD_DIM)
    steps = step_size.reshape(DEVICES, SUF, SSM_HEADS)
    bmap = state_in.reshape(DEVICES, SUF, NS)
    cmap = state_out.reshape(DEVICES, SUF, NS)

    def advance(carry, slices):
        x_t, dt_t, b_t, c_t = slices
        factor = jnp.exp(-decay_rate[None, :] * dt_t)
        carry = factor[:, None, :, None] * carry + b_t[:, :, None, None] * (dt_t[:, :, None] * x_t)[:, None]
        y_t = jnp.einsum("rn,rnhp->rhp", c_t, carry, precision=lax.Precision.HIGHEST) + skip_gain[None, :, None] * x_t
        return carry, y_t

    slices = (jnp.swapaxes(inputs, 0, 1), jnp.swapaxes(steps, 0, 1), jnp.swapaxes(bmap, 0, 1), jnp.swapaxes(cmap, 0, 1))
    final, outputs = lax.scan(advance, state, slices)
    mixed = jnp.swapaxes(outputs, 0, 1).reshape(TOKENS, DI).astype(jnp.bfloat16)
    return attended, mixed
```

```python
import jax
import jax.numpy as jnp
from jax import lax
from jax.experimental import pallas as pl
from jax.experimental.pallas import tpu as pltpu
from jax.sharding import PartitionSpec as P

KV_HEADS = 8
HEAD_DIM = 128
SSM_HEAD_DIM = 64
BLK = 16
MIX_BLOCK = 512
AHEAD = 3
MESH = pl.DeviceIdType.MESH
N_ALL = 128
F32 = jnp.float32
BF16 = jnp.bfloat16


def place():
    g = lax.axis_index("grp")
    d = lax.axis_index("dev")
    return g, d // 8, (d // 2) % 4, d % 2


def shifted(i):
    a, b, c = i % 4, (i // 4) % 4, (i // 16) % 4
    return a, a + b, a + c, i // 64


def partner(i):
    g, y, z, core = place()
    a, b, c, e = shifted(i)
    return (g + a) % 4, (((y + b) % 4) * 4 + (z + c) % 4) * 2 + (core + e) % 2


def split(values):
    high = values.astype(BF16)
    return high, (values - high.astype(F32)).astype(BF16)


def exact_dot(a, b, dims):
    return lax.dot_general(
        a, b, (dims, ((), ())), precision=lax.Precision.HIGHEST, preferred_element_type=F32
    )


def dot(a, b, dims=((1,), (0,))):
    return lax.dot_general(a, b, (dims, ((), ())), preferred_element_type=F32)


def kernel(
    codes,
    own,
    wanted,
    steps,
    decay,
    in_map,
    out_map,
    skip,
    queries_hbm,
    new_hbm,
    pool_hbm,
    inputs_hbm,
    states_hbm,
    attended_hbm,
    mixed_hbm,
    pool,
    states,
    queries,
    new,
    inputs,
    staged,
    arrived,
    state_out,
    state_in,
    attended,
    mixed,
    bias,
    rise_pair,
    fall_pair,
    skip_pair,
    inter_high,
    inter_low,
    out_pair,
    load_sem,
    send_sem,
    recv_sem,
    state_send_sem,
    state_recv_sem,
    out_sem,
):
    g, y, z, core = place()
    dev = lax.axis_index("dev")
    me = g * 32 + dev
    loads = [
        pltpu.make_async_copy(source, target, load_sem.at[n])
        for n, (source, target) in enumerate(
            (
                (states_hbm, states),
                (pool_hbm, pool),
                (inputs_hbm, inputs),
                (queries_hbm, queries),
                (new_hbm, new),
            )
        )
    ]
    for load in loads:
        load.start()

    barrier = pltpu.get_barrier_semaphore()

    def greet(i, carry):
        pl.semaphore_signal(barrier, inc=1, device_id=partner(i), device_id_type=MESH)
        return carry

    lax.fori_loop(1, N_ALL, greet, 0)

    loads[0].wait()
    for k in range(1, 4):
        slot = jnp.maximum(codes[((g + k) % 4) * 32 + dev] // 128 - 1, 0)
        state_out[k - 1] = states[slot].astype(BF16)
    state_in[3] = states[jnp.maximum(codes[me] // 128 - 1, 0)].astype(BF16)
    loads[1].wait()

    def stage(i, carry):
        pg, pd = partner(i)
        block = pool[jnp.clip(codes[pg * 32 + pd] % 128 - 1, 0, 63)]
        for c in range(KV_HEADS):
            staged[c, i - 1, :, :HEAD_DIM] = block[:, c * HEAD_DIM : (c + 1) * HEAD_DIM]
            staged[c, i - 1, :, HEAD_DIM:] = block[:, (8 + c) * HEAD_DIM : (9 + c) * HEAD_DIM]
        return carry

    lax.fori_loop(1, N_ALL, stage, 0)
    block = pool[jnp.clip(codes[me] % 128 - 1, 0, 63)]
    for c in range(KV_HEADS):
        arrived[c, 127, :, :HEAD_DIM] = block[:, c * HEAD_DIM : (c + 1) * HEAD_DIM]
        arrived[c, 127, :, HEAD_DIM:] = block[:, (8 + c) * HEAD_DIM : (9 + c) * HEAD_DIM]

    pl.semaphore_wait(barrier, N_ALL - 1)

    for k in range(1, 4):
        pltpu.make_async_remote_copy(
            state_out.at[k - 1],
            state_in.at[k - 1],
            state_send_sem,
            state_recv_sem,
            device_id=((g + k) % 4, dev),
            device_id_type=MESH,
        ).start()

    def send(c):
        def one(i, carry):
            pltpu.make_async_remote_copy(
                staged.at[c, i - 1],
                arrived.at[c, i - 1],
                send_sem.at[c],
                recv_sem.at[c],
                device_id=partner(i),
                device_id_type=MESH,
            ).start()
            return carry

        lax.fori_loop(1, N_ALL, one, 0)

    for c in range(AHEAD):
        send(c)

    suffix = steps.shape[0]
    rows = lax.broadcasted_iota(jnp.int32, (suffix, suffix), 0)
    lower = rows >= lax.broadcasted_iota(jnp.int32, (suffix, suffix), 1)
    total = exact_dot(jnp.where(lower, 1.0, 0.0), steps[...] * decay[...], ((1,), (0,)))
    heads = total.shape[1]
    high, low = split(jnp.exp(-total))
    rise_pair[:, :heads] = high
    rise_pair[:, heads:] = low
    high, low = split(jnp.exp(total) * steps[...])
    fall_pair[:, :heads] = high
    fall_pair[:, heads:] = low
    high, low = split(jnp.broadcast_to(skip[...], (16, heads)))
    skip_pair[:, :heads] = high
    skip_pair[:, heads:] = low
    inter = jnp.where(lower, exact_dot(out_map[...], in_map[...], ((1,), (1,))), 0.0)
    high, low = split(inter)
    inter_high[...] = high
    inter_low[...] = low
    high, low = split(out_map[...])
    out_pair[...] = jnp.concatenate([high, low], axis=1)

    holder = lax.broadcasted_iota(jnp.int32, (N_ALL, N_ALL * BLK), 0)
    offset = lax.broadcasted_iota(jnp.int32, (N_ALL, N_ALL * BLK), 1) // BLK + 1
    a, b, c, e = shifted(offset % N_ALL)
    source = ((g + 8 - a) % 4) * 32 + ((y + 8 - b) % 4) * 8 + ((z + 8 - c) % 4) * 2 + (core + e) % 2
    chosen = jnp.where(holder == source, 1.0, 0.0).astype(BF16)
    live = jnp.where(wanted[...] >= 0, 1.0, 0.0).astype(BF16)
    seen = dot(jnp.broadcast_to(live, (16, N_ALL)), chosen)
    bias[...] = jnp.where(seen[:8] > 0.5, 0.0, -1e30)

    pltpu.make_async_copy(state_out, state_in.at[0:3], state_recv_sem).wait()
    loads[2].wait()
    which = (g - own[0] + 7) % 4

    def mix(j, carry):
        columns = pl.ds(pl.multiple_of(j * MIX_BLOCK, MIX_BLOCK), MIX_BLOCK)
        row = lax.broadcasted_iota(jnp.int32, (2 * heads, MIX_BLOCK), 0) % heads
        head = (lax.broadcasted_iota(jnp.int32, (2 * heads, MIX_BLOCK), 1) + j * MIX_BLOCK) // SSM_HEAD_DIM
        spread = jnp.where(row == head, 1.0, 0.0).astype(BF16)
        values = inputs[:, columns].astype(F32)
        high, low = split(dot(fall_pair[...], spread) * values)
        start = state_in[which, :, columns]
        inner = dot(inter_high[...], high) + dot(inter_low[...], high) + dot(inter_high[...], low)
        inner = inner + dot(out_pair[...], jnp.concatenate([start, start], axis=0))
        result = dot(rise_pair[...], spread) * inner + dot(skip_pair[...], spread)[:1] * values
        mixed[:, columns] = result.astype(BF16)
        return carry

    lax.fori_loop(0, inputs.shape[1] // MIX_BLOCK, mix, 0)
    store_mixed = pltpu.make_async_copy(mixed, mixed_hbm, out_sem.at[0])
    store_mixed.start()

    loads[3].wait()
    loads[4].wait()
    group = queries.shape[1] // (KV_HEADS * HEAD_DIM)
    scale = HEAD_DIM ** (-0.5)
    width = group * HEAD_DIM

    def store_of(c):
        columns = pl.ds(pl.multiple_of(c * width, width), width)
        return pltpu.make_async_copy(
            attended.at[:, columns], attended_hbm.at[:, columns], out_sem.at[1]
        )

    def attend(c, carry):
        pltpu.make_async_copy(
            staged.at[c, 0 : N_ALL - 1], arrived.at[c, 0 : N_ALL - 1], recv_sem.at[c]
        ).wait()
        keys = arrived[c, :, :, :HEAD_DIM].reshape(N_ALL * BLK, HEAD_DIM)
        values = arrived[c, :, :, HEAD_DIM:].reshape(N_ALL * BLK, HEAD_DIM)
        keys_new = new[:, pl.ds(pl.multiple_of(c * HEAD_DIM, HEAD_DIM), HEAD_DIM)]
        values_new = new[:, pl.ds(pl.multiple_of((c + 8) * HEAD_DIM, HEAD_DIM), HEAD_DIM)]

        def one(h, carry):
            columns = pl.ds(pl.multiple_of((c * group + h) * HEAD_DIM, HEAD_DIM), HEAD_DIM)
            query = queries[:, columns]
            old = dot(query, keys, ((1,), (1,))) * scale + bias[0:1]
            fresh = jnp.where(lower, dot(query, keys_new, ((1,), (1,))) * scale, -1e30)
            peak = jnp.maximum(
                jnp.max(old, axis=1, keepdims=True), jnp.max(fresh, axis=1, keepdims=True)
            )
            old = jnp.exp(old - peak)
            fresh = jnp.exp(fresh - peak)
            weight = jnp.sum(old, axis=1, keepdims=True) + jnp.sum(fresh, axis=1, keepdims=True)
            result = dot(old.astype(BF16), values) + dot(fresh.astype(BF16), values_new)
            attended[:, columns] = (result / weight).astype(BF16)
            return carry

        lax.fori_loop(0, group, one, 0)
        store_of(c).start()

        @pl.when(c + AHEAD < KV_HEADS)
        def _():
            send(c + AHEAD)

        return carry

    lax.fori_loop(0, KV_HEADS, attend, 0)

    pltpu.make_async_copy(attended, attended_hbm, out_sem.at[1]).wait()
    store_mixed.wait()
    pltpu.make_async_copy(state_out, state_in.at[0:3], state_send_sem).wait()
    for c in range(KV_HEADS):
        pltpu.make_async_copy(
            staged.at[c, 0 : N_ALL - 1], arrived.at[c, 0 : N_ALL - 1], send_sem.at[c]
        ).wait()


def body(
    queries,
    new_kv,
    kv_pool,
    hit_holder,
    hit_block,
    hit_count,
    ssm_input,
    step_size,
    decay_rate,
    state_in,
    state_out,
    skip_gain,
    state_pool,
    state_group,
    state_slot,
):
    n_all = lax.axis_size(("grp", "dev"))
    n_dev = lax.axis_size("dev")
    holders = jnp.arange(n_all, dtype=jnp.int32)
    entries = jnp.arange(hit_holder.shape[1], dtype=jnp.int32)
    chosen = (hit_holder[0][:, None] == holders[None, :]) & (entries[:, None] < hit_count[0])
    wanted = jnp.sum(jnp.where(chosen, hit_block[0][:, None] + 1, 0), axis=0) - 1
    state_holder = state_group[0] * n_dev + lax.axis_index("dev")
    asked_state = jnp.where(holders == state_holder, state_slot[0] + 1, 0)
    codes = lax.all_to_all(
        (wanted + 1 + 128 * asked_state).reshape(n_all, 1),
        ("grp", "dev"),
        split_axis=0,
        concat_axis=0,
        tiled=True,
    )[:, 0]

    suffix, channels = ssm_input.shape
    heads = decay_rate.shape[0]
    states = state_in.shape[1]
    smem = pl.BlockSpec(memory_space=pltpu.SMEM)
    vmem = pl.BlockSpec(memory_space=pltpu.VMEM)
    left = pl.BlockSpec(memory_space=pl.ANY)
    return pl.pallas_call(
        kernel,
        name="prefill",
        out_shape=(
            jax.ShapeDtypeStruct(queries.shape, BF16),
            jax.ShapeDtypeStruct(ssm_input.shape, BF16),
        ),
        in_specs=[smem] * 2 + [vmem] * 6 + [left] * 5,
        out_specs=(left, left),
        scratch_shapes=[
            pltpu.VMEM(kv_pool.shape, BF16),
            pltpu.VMEM(state_pool.shape, F32),
            pltpu.VMEM(queries.shape, BF16),
            pltpu.VMEM(new_kv.shape, BF16),
            pltpu.VMEM(ssm_input.shape, BF16),
            pltpu.VMEM((KV_HEADS, n_all, BLK, 2 * HEAD_DIM), BF16),
            pltpu.VMEM((KV_HEADS, n_all, BLK, 2 * HEAD_DIM), BF16),
            pltpu.VMEM((3, states, channels), BF16),
            pltpu.VMEM((4, states, channels), BF16),
            pltpu.VMEM(queries.shape, BF16),
            pltpu.VMEM(ssm_input.shape, BF16),
            pltpu.VMEM((8, n_all * BLK), F32),
            pltpu.VMEM((suffix, 2 * heads), BF16),
            pltpu.VMEM((suffix, 2 * heads), BF16),
            pltpu.VMEM((16, 2 * heads), BF16),
            pltpu.VMEM((suffix, suffix), BF16),
            pltpu.VMEM((suffix, suffix), BF16),
            pltpu.VMEM((suffix, 2 * states), BF16),
            pltpu.SemaphoreType.DMA((5,)),
            pltpu.SemaphoreType.DMA((KV_HEADS,)),
            pltpu.SemaphoreType.DMA((KV_HEADS,)),
            pltpu.SemaphoreType.DMA,
            pltpu.SemaphoreType.DMA,
            pltpu.SemaphoreType.DMA((2,)),
        ],
        compiler_params=pltpu.CompilerParams(
            collective_id=0, has_side_effects=True, vmem_limit_bytes=63 * 2**20
        ),
    )(
        codes,
        state_group,
        wanted[None, :],
        step_size,
        decay_rate[None, :],
        state_in,
        state_out,
        skip_gain[None, :],
        queries,
        new_kv,
        kv_pool,
        ssm_input,
        state_pool,
    )


def solution(mesh):
    return jax.shard_map(
        body,
        mesh=mesh,
        in_specs=(
            P(("grp", "dev"), None),
            P(("grp", "dev"), None),
            P(("grp", "dev"), None, None),
            P(("grp", "dev"), None),
            P(("grp", "dev"), None),
            P(("grp", "dev")),
            P(("grp", "dev"), None),
            P(("grp", "dev"), None),
            P(),
            P(("grp", "dev"), None),
            P(("grp", "dev"), None),
            P(),
            P(("grp", "dev"), None, None),
            P(("grp", "dev")),
            P(("grp", "dev")),
        ),
        out_specs=(P(("grp", "dev"), None), P(("grp", "dev"), None)),
        check_vma=False,
    )
```

```python
import jax
import jax.numpy as jnp
from jax import lax
from jax.experimental import pallas as pl
from jax.experimental.pallas import tpu as pltpu
from jax.sharding import PartitionSpec as P

KV_HEADS = 8
HEAD_DIM = 128
SSM_HEAD_DIM = 64
BLK = 16
MIX_BLOCK = 512
AHEAD = 3
VMEM_LIMIT = 48 * 2**20
MESH = pl.DeviceIdType.MESH
N_ALL = 128
F32 = jnp.float32
BF16 = jnp.bfloat16


def place():
    g = lax.axis_index("grp")
    d = lax.axis_index("dev")
    return g, lax.div(d, 8), lax.rem(lax.div(d, 2), 4), lax.rem(d, 2)


def shifted(i):
    a, b, c = lax.rem(i, 4), lax.rem(lax.div(i, 4), 4), lax.rem(lax.div(i, 16), 4)
    return a, lax.rem(a + b, 4), lax.rem(a + c, 4), lax.div(i, 64)


def at(a, b, c, e):
    g, y, z, core = place()
    dev = (lax.rem(y + b, 4) * 4 + lax.rem(z + c, 4)) * 2 + lax.rem(core + e, 2)
    return lax.rem(g + a, 4), dev


def partner(i):
    return at(*shifted(i))


def gathered_row(a, b, c, e):
    back_a, back_b, back_c = lax.rem(4 - a, 4), lax.rem(4 - b, 4), lax.rem(4 - c, 4)
    return (back_b * 4 + back_c) * 8 + back_a * 2 + e


def split(values):
    high = values.astype(BF16)
    return high, (values - high.astype(F32)).astype(BF16)


def exact_dot(a, b, dims):
    return lax.dot_general(
        a, b, (dims, ((), ())), precision=lax.Precision.HIGHEST, preferred_element_type=F32
    )


def dot(a, b, dims=((1,), (0,))):
    return lax.dot_general(a, b, (dims, ((), ())), preferred_element_type=F32)


def kernel(
    state_group,
    state_slot,
    hit_count,
    hit_holder,
    hit_block,
    steps,
    decay,
    in_map,
    out_map,
    skip,
    queries_hbm,
    new_hbm,
    pool_hbm,
    inputs_hbm,
    states_hbm,
    attended,
    mixed,
    pool,
    states,
    queries,
    new,
    inputs,
    staged,
    arrived,
    state_out,
    state_in,
    asked,
    asked_near,
    asked_all,
    bias,
    rise_pair,
    fall_pair,
    skip_pair,
    inter_high,
    inter_low,
    out_pair,
    load_sem,
    send_sem,
    recv_sem,
    state_send_sem,
    state_recv_sem,
    ask_send_sem,
    ask_recv_sem,
    ask_sem,
):
    g, y, z, core = place()
    dev = lax.axis_index("dev")
    me = g * 32 + dev
    loads = [
        pltpu.make_async_copy(source, target, load_sem.at[n])
        for n, (source, target) in enumerate(
            (
                (states_hbm, states),
                (pool_hbm, pool),
                (inputs_hbm, inputs),
                (queries_hbm, queries),
                (new_hbm, new),
            )
        )
    ]
    for load in loads:
        load.start()

    barrier = pltpu.get_barrier_semaphore()
    near = [(a, e) for a in (2, 1, 3, 0) for e in (1, 0) if (a, e) != (0, 0)]
    plane = [(b, c) for b in (2, 1, 3, 0) for c in (2, 1, 3, 0) if (b, c) != (0, 0)]
    for offset in [(a, 0, 0, e) for a, e in near] + [(0, b, c, 0) for b, c in plane]:
        pl.semaphore_signal(barrier, inc=1, device_id=at(*offset), device_id_type=MESH)

    entries = hit_holder.shape[1]
    entry = lax.broadcasted_iota(jnp.int32, (1, entries), 1)
    holder = jnp.where(entry < hit_count[0], hit_holder[...], -1)
    held = lax.broadcasted_iota(jnp.int32, (N_ALL, entries), 0) == holder
    numbers = jnp.broadcast_to((hit_block[...] + 1).astype(F32), (8, entries))
    wanted = exact_dot(numbers, jnp.where(held, 1.0, 0.0), ((1,), (1,)))[:1]
    lane = lax.broadcasted_iota(jnp.int32, (1, N_ALL), 1)
    asked_state = jnp.where(lane == state_group[0] * 32 + dev, state_slot[0] + 1, 0)
    asked[0] = (wanted + 0.5).astype(jnp.int32) + 128 * asked_state

    pl.semaphore_wait(barrier, len(near) + len(plane))
    for a, e in near:
        pltpu.make_async_remote_copy(
            asked.at[pl.ds(0, 1)],
            asked.at[pl.ds(a * 2 + e, 1)],
            ask_send_sem.at[0],
            ask_recv_sem.at[0],
            device_id=at(a, 0, 0, e),
            device_id_type=MESH,
        ).start()
    first = pltpu.make_async_copy(asked.at[pl.ds(0, 7)], asked.at[pl.ds(1, 7)], ask_recv_sem.at[0])
    first.wait()
    for b, c in plane:
        pltpu.make_async_remote_copy(
            asked.at[pl.ds(0, 8)],
            asked.at[pl.ds((b * 4 + c) * 8, 8)],
            ask_send_sem.at[1],
            ask_recv_sem.at[1],
            device_id=at(0, b, c, 0),
            device_id_type=MESH,
        ).start()

    copy_near = pltpu.make_async_copy(asked.at[pl.ds(0, 8)], asked_near, ask_sem)
    copy_near.start()
    copy_near.wait()
    loads[0].wait()

    def slot_for(row):
        return jnp.clip(lax.div(asked_near[row, 0, me], 128) - 1, 0, 1)

    for k in range(1, 4):
        state_out[k - 1] = states[slot_for(gathered_row(k, 0, 0, 0))].astype(BF16)
    state_in[3] = states[slot_for(0)].astype(BF16)
    for k in range(1, 4):
        pltpu.make_async_remote_copy(
            state_out.at[k - 1],
            state_in.at[k - 1],
            state_send_sem,
            state_recv_sem,
            device_id=at(k, 0, 0, 0),
            device_id_type=MESH,
        ).start()

    second = pltpu.make_async_copy(
        asked.at[pl.ds(0, 120)], asked.at[pl.ds(8, 120)], ask_recv_sem.at[1]
    )
    second.wait()
    copy_all = pltpu.make_async_copy(asked, asked_all, ask_sem)
    copy_all.start()
    copy_all.wait()
    loads[1].wait()

    def block_for(row):
        return jnp.clip(lax.rem(asked_all[row, 0, me], 128) - 1, 0, 63)

    def stage(i, carry):
        block = pool[block_for(gathered_row(*shifted(i)))]
        for c in range(KV_HEADS):
            staged[c, i - 1, :, :HEAD_DIM] = block[:, c * HEAD_DIM : (c + 1) * HEAD_DIM]
            staged[c, i - 1, :, HEAD_DIM:] = block[:, (8 + c) * HEAD_DIM : (9 + c) * HEAD_DIM]
        return carry

    lax.fori_loop(1, N_ALL, stage, 0)
    block = pool[block_for(0)]
    for c in range(KV_HEADS):
        arrived[c, 127, :, :HEAD_DIM] = block[:, c * HEAD_DIM : (c + 1) * HEAD_DIM]
        arrived[c, 127, :, HEAD_DIM:] = block[:, (8 + c) * HEAD_DIM : (9 + c) * HEAD_DIM]

    def send(c):
        def one(i, carry):
            pltpu.make_async_remote_copy(
                staged.at[c, i - 1],
                arrived.at[c, i - 1],
                send_sem.at[c],
                recv_sem.at[c],
                device_id=partner(i),
                device_id_type=MESH,
            ).start()
            return carry

        lax.fori_loop(1, N_ALL, one, 0)

    for c in range(AHEAD):
        send(c)

    suffix = steps.shape[0]
    rows = lax.broadcasted_iota(jnp.int32, (suffix, suffix), 0)
    lower = rows >= lax.broadcasted_iota(jnp.int32, (suffix, suffix), 1)
    total = exact_dot(jnp.where(lower, 1.0, 0.0), steps[...] * decay[...], ((1,), (0,)))
    heads = total.shape[1]
    high, low = split(jnp.exp(-total))
    rise_pair[:, :heads] = high
    rise_pair[:, heads:] = low
    high, low = split(jnp.exp(total) * steps[...])
    fall_pair[:, :heads] = high
    fall_pair[:, heads:] = low
    high, low = split(jnp.broadcast_to(skip[...], (16, heads)))
    skip_pair[:, :heads] = high
    skip_pair[:, heads:] = low
    inter = jnp.where(lower, exact_dot(out_map[...], in_map[...], ((0,), (0,))), 0.0)
    high, low = split(inter)
    inter_high[...] = high
    inter_low[...] = low
    high, low = split(out_map[...])
    out_pair[...] = jnp.concatenate([high, low], axis=0)

    holder = lax.broadcasted_iota(jnp.int32, (N_ALL, N_ALL * BLK), 0)
    offset = lax.broadcasted_iota(jnp.int32, (N_ALL, N_ALL * BLK), 1) // BLK + 1
    a, b, c, e = shifted(offset % N_ALL)
    source = ((g + 4 - a) % 4) * 32 + ((y + 4 - b) % 4) * 8 + ((z + 4 - c) % 4) * 2 + (core + e) % 2
    chosen = jnp.where(holder == source, 1.0, 0.0).astype(BF16)
    live = jnp.where(wanted > 0.5, 1.0, 0.0).astype(BF16)
    seen = dot(jnp.broadcast_to(live, (16, N_ALL)), chosen)
    bias[...] = jnp.where(seen[:8] > 0.5, 0.0, -1e30)

    pltpu.make_async_copy(state_out, state_in.at[0:3], state_recv_sem).wait()
    loads[2].wait()
    which = lax.rem(g - state_group[0] + 7, 4)

    def mix(j, carry):
        columns = pl.ds(pl.multiple_of(j * MIX_BLOCK, MIX_BLOCK), MIX_BLOCK)
        row = lax.broadcasted_iota(jnp.int32, (2 * heads, MIX_BLOCK), 0) % heads
        head = (lax.broadcasted_iota(jnp.int32, (2 * heads, MIX_BLOCK), 1) + j * MIX_BLOCK) // SSM_HEAD_DIM
        spread = jnp.where(row == head, 1.0, 0.0).astype(BF16)
        values = inputs[:, columns].astype(F32)
        high, low = split(dot(fall_pair[...], spread) * values)
        start = state_in[which, :, columns]
        inner = dot(inter_high[...], high) + dot(inter_low[...], high) + dot(inter_high[...], low)
        inner = inner + dot(out_pair[...], jnp.concatenate([start, start], axis=0), ((0,), (0,)))
        result = dot(rise_pair[...], spread) * inner + dot(skip_pair[...], spread)[:1] * values
        mixed[:, columns] = result.astype(BF16)
        return carry

    lax.fori_loop(0, inputs.shape[1] // MIX_BLOCK, mix, 0)

    loads[3].wait()
    loads[4].wait()
    group = queries.shape[1] // (KV_HEADS * HEAD_DIM)
    scale = HEAD_DIM ** (-0.5)

    def attend(c, carry):
        pltpu.make_async_copy(
            staged.at[c, 0 : N_ALL - 1], arrived.at[c, 0 : N_ALL - 1], recv_sem.at[c]
        ).wait()
        keys = arrived[c, :, :, :HEAD_DIM].reshape(N_ALL * BLK, HEAD_DIM)
        values = arrived[c, :, :, HEAD_DIM:].reshape(N_ALL * BLK, HEAD_DIM)
        keys_new = new[:, pl.ds(pl.multiple_of(c * HEAD_DIM, HEAD_DIM), HEAD_DIM)]
        values_new = new[:, pl.ds(pl.multiple_of((c + 8) * HEAD_DIM, HEAD_DIM), HEAD_DIM)]

        def one(h, carry):
            columns = pl.ds(pl.multiple_of((c * group + h) * HEAD_DIM, HEAD_DIM), HEAD_DIM)
            query = queries[:, columns]
            old = dot(query, keys, ((1,), (1,))) * scale + bias[0:1]
            fresh = jnp.where(lower, dot(query, keys_new, ((1,), (1,))) * scale, -1e30)
            peak = jnp.maximum(
                jnp.max(old, axis=1, keepdims=True), jnp.max(fresh, axis=1, keepdims=True)
            )
            old = jnp.exp(old - peak)
            fresh = jnp.exp(fresh - peak)
            weight = jnp.sum(old, axis=1, keepdims=True) + jnp.sum(fresh, axis=1, keepdims=True)
            result = dot(old.astype(BF16), values) + dot(fresh.astype(BF16), values_new)
            attended[:, columns] = (result / weight).astype(BF16)
            return carry

        lax.fori_loop(0, group, one, 0)

        @pl.when(c + AHEAD < KV_HEADS)
        def _():
            send(c + AHEAD)

        return carry

    lax.fori_loop(0, KV_HEADS, attend, 0)

    pltpu.make_async_copy(asked.at[pl.ds(0, 7)], asked.at[pl.ds(1, 7)], ask_send_sem.at[0]).wait()
    pltpu.make_async_copy(
        asked.at[pl.ds(0, 120)], asked.at[pl.ds(8, 120)], ask_send_sem.at[1]
    ).wait()
    pltpu.make_async_copy(state_out, state_in.at[0:3], state_send_sem).wait()
    for c in range(KV_HEADS):
        pltpu.make_async_copy(
            staged.at[c, 0 : N_ALL - 1], arrived.at[c, 0 : N_ALL - 1], send_sem.at[c]
        ).wait()


def body(
    queries,
    new_kv,
    kv_pool,
    hit_holder,
    hit_block,
    hit_count,
    ssm_input,
    step_size,
    decay_rate,
    state_in,
    state_out,
    skip_gain,
    state_pool,
    state_group,
    state_slot,
):
    n_all = lax.axis_size(("grp", "dev"))
    suffix, channels = ssm_input.shape
    heads = decay_rate.shape[0]
    states = state_in.shape[1]
    smem = pl.BlockSpec(memory_space=pltpu.SMEM)
    vmem = pl.BlockSpec(memory_space=pltpu.VMEM)
    left = pl.BlockSpec(memory_space=pl.ANY)
    return pl.pallas_call(
        kernel,
        name="prefill",
        out_shape=(
            pltpu.VMEM(queries.shape, BF16),
            pltpu.VMEM(ssm_input.shape, BF16),
        ),
        in_specs=[smem] * 3 + [vmem] * 7 + [left] * 5,
        out_specs=(vmem, vmem),
        scratch_shapes=[
            pltpu.VMEM(kv_pool.shape, BF16),
            pltpu.VMEM(state_pool.shape, F32),
            pltpu.VMEM(queries.shape, BF16),
            pltpu.VMEM(new_kv.shape, BF16),
            pltpu.VMEM(ssm_input.shape, BF16),
            pltpu.VMEM((KV_HEADS, n_all, BLK, 2 * HEAD_DIM), BF16),
            pltpu.VMEM((KV_HEADS, n_all, BLK, 2 * HEAD_DIM), BF16),
            pltpu.VMEM((3, states, channels), BF16),
            pltpu.VMEM((4, states, channels), BF16),
            pltpu.VMEM((n_all, 1, n_all), jnp.int32),
            pltpu.SMEM((8, 1, n_all), jnp.int32),
            pltpu.SMEM((n_all, 1, n_all), jnp.int32),
            pltpu.VMEM((8, n_all * BLK), F32),
            pltpu.VMEM((suffix, 2 * heads), BF16),
            pltpu.VMEM((suffix, 2 * heads), BF16),
            pltpu.VMEM((16, 2 * heads), BF16),
            pltpu.VMEM((suffix, suffix), BF16),
            pltpu.VMEM((suffix, suffix), BF16),
            pltpu.VMEM((2 * states, suffix), BF16),
            pltpu.SemaphoreType.DMA((5,)),
            pltpu.SemaphoreType.DMA((KV_HEADS,)),
            pltpu.SemaphoreType.DMA((KV_HEADS,)),
            pltpu.SemaphoreType.DMA,
            pltpu.SemaphoreType.DMA,
            pltpu.SemaphoreType.DMA((2,)),
            pltpu.SemaphoreType.DMA((2,)),
            pltpu.SemaphoreType.DMA,
        ],
        compiler_params=pltpu.CompilerParams(
            collective_id=0, has_side_effects=True, vmem_limit_bytes=VMEM_LIMIT
        ),
    )(
        state_group,
        state_slot,
        hit_count,
        hit_holder,
        hit_block,
        step_size,
        decay_rate[None, :],
        state_in.T,
        state_out.T,
        skip_gain[None, :],
        queries,
        new_kv,
        kv_pool,
        ssm_input,
        state_pool,
    )


def solution(mesh):
    return jax.shard_map(
        body,
        mesh=mesh,
        in_specs=(
            P(("grp", "dev"), None),
            P(("grp", "dev"), None),
            P(("grp", "dev"), None, None),
            P(("grp", "dev"), None),
            P(("grp", "dev"), None),
            P(("grp", "dev")),
            P(("grp", "dev"), None),
            P(("grp", "dev"), None),
            P(),
            P(("grp", "dev"), None),
            P(("grp", "dev"), None),
            P(),
            P(("grp", "dev"), None, None),
            P(("grp", "dev")),
            P(("grp", "dev")),
        ),
        out_specs=(P(("grp", "dev"), None), P(("grp", "dev"), None)),
        check_vma=False,
    )
```

```python
import jax
import jax.numpy as jnp
from jax import lax
from jax.experimental import pallas as pl
from jax.experimental.pallas import tpu as pltpu
from jax.sharding import PartitionSpec as P

KV_HEADS = 8
HEAD_DIM = 128
SSM_HEAD_DIM = 64
BLK = 16
MIX_BLOCK = 512
AHEAD = 3
VMEM_LIMIT = 48 * 2**20
MESH = pl.DeviceIdType.MESH
N_ALL = 128
F32 = jnp.float32
BF16 = jnp.bfloat16


def place():
    g = lax.axis_index("grp")
    d = lax.axis_index("dev")
    return g, lax.div(d, 8), lax.rem(lax.div(d, 2), 4), lax.rem(d, 2)


def shifted(i):
    a, b, c = lax.rem(i, 4), lax.rem(lax.div(i, 4), 4), lax.rem(lax.div(i, 16), 4)
    return a, lax.rem(a + b, 4), lax.rem(a + c, 4), lax.div(i, 64)


def at(a, b, c, e):
    g, y, z, core = place()
    dev = (lax.rem(y + b, 4) * 4 + lax.rem(z + c, 4)) * 2 + lax.rem(core + e, 2)
    return lax.rem(g + a, 4), dev


def partner(i):
    return at(*shifted(i))


def gathered_row(a, b, c, e):
    back_a, back_b, back_c = lax.rem(4 - a, 4), lax.rem(4 - b, 4), lax.rem(4 - c, 4)
    return (back_b * 4 + back_c) * 8 + back_a * 2 + e


def split(values):
    high = values.astype(BF16)
    return high, (values - high.astype(F32)).astype(BF16)


def exact_dot(a, b, dims):
    return lax.dot_general(
        a, b, (dims, ((), ())), precision=lax.Precision.HIGHEST, preferred_element_type=F32
    )


def dot(a, b, dims=((1,), (0,))):
    return lax.dot_general(a, b, (dims, ((), ())), preferred_element_type=F32)


def kernel(
    state_group,
    state_slot,
    hit_count,
    hit_holder,
    hit_block,
    steps,
    decay,
    in_map,
    out_map,
    skip,
    queries_hbm,
    new_hbm,
    pool_hbm,
    inputs_hbm,
    states_hbm,
    attended,
    mixed,
    pool,
    states,
    queries,
    new,
    inputs,
    staged,
    arrived,
    staged_last,
    arrived_last,
    state_out,
    state_in,
    asked,
    asked_all,
    weights,
    partial,
    rounded,
    bias,
    rise_pair,
    fall_pair,
    skip_pair,
    inter_high,
    inter_low,
    out_pair,
    load_sem,
    send_sem,
    recv_sem,
    state_send_sem,
    state_recv_sem,
    ask_send_sem,
    ask_recv_sem,
    ask_sem,
):
    g, y, z, core = place()
    dev = lax.axis_index("dev")
    me = g * 32 + dev
    loads = [
        pltpu.make_async_copy(source, target, load_sem.at[n])
        for n, (source, target) in enumerate(
            (
                (states_hbm, states),
                (pool_hbm, pool),
                (inputs_hbm, inputs),
                (queries_hbm, queries),
                (new_hbm, new),
            )
        )
    ]
    for load in loads:
        load.start()

    barrier = pltpu.get_barrier_semaphore()
    near = [(a, e) for a in (2, 1, 3, 0) for e in (1, 0) if (a, e) != (0, 0)]
    plane = [(b, c) for b in (2, 1, 3, 0) for c in (2, 1, 3, 0) if (b, c) != (0, 0)]
    for offset in [(a, 0, 0, e) for a, e in near] + [(0, b, c, 0) for b, c in plane]:
        pl.semaphore_signal(barrier, inc=1, device_id=at(*offset), device_id_type=MESH)

    entries = hit_holder.shape[1]
    entry = lax.broadcasted_iota(jnp.int32, (1, entries), 1)
    holder = jnp.where(entry < hit_count[0], hit_holder[...], -1)
    held = lax.broadcasted_iota(jnp.int32, (N_ALL, entries), 0) == holder
    numbers = jnp.broadcast_to((hit_block[...] + 1).astype(F32), (8, entries))
    wanted = exact_dot(numbers, jnp.where(held, 1.0, 0.0), ((1,), (1,)))[:1]
    lane = lax.broadcasted_iota(jnp.int32, (1, N_ALL), 1)
    asked_state = jnp.where(lane == state_group[0] * 32 + dev, state_slot[0] + 1, 0)
    asked[0] = (wanted + 0.5).astype(jnp.int32) + 128 * asked_state

    pl.semaphore_wait(barrier, len(near) + len(plane))
    for a, e in near:
        pltpu.make_async_remote_copy(
            asked.at[pl.ds(0, 1)],
            asked.at[pl.ds(a * 2 + e, 1)],
            ask_send_sem.at[0],
            ask_recv_sem.at[0],
            device_id=at(a, 0, 0, e),
            device_id_type=MESH,
        ).start()
    first = pltpu.make_async_copy(asked.at[pl.ds(0, 7)], asked.at[pl.ds(1, 7)], ask_recv_sem.at[0])
    first.wait()
    for b, c in plane:
        pltpu.make_async_remote_copy(
            asked.at[pl.ds(0, 8)],
            asked.at[pl.ds((b * 4 + c) * 8, 8)],
            ask_send_sem.at[1],
            ask_recv_sem.at[1],
            device_id=at(0, b, c, 0),
            device_id_type=MESH,
        ).start()

    loads[0].wait()

    def state_for(row):
        code = jnp.sum(jnp.where(lane == me, asked[row], 0), axis=1, keepdims=True)
        return jnp.where(code >= 256, states[1], states[0]).astype(BF16)

    for k in range(1, 4):
        state_out[k - 1] = state_for(gathered_row(k, 0, 0, 0))
    state_in[3] = state_for(0)
    for k in range(1, 4):
        pltpu.make_async_remote_copy(
            state_out.at[k - 1],
            state_in.at[k - 1],
            state_send_sem,
            state_recv_sem,
            device_id=at(k, 0, 0, 0),
            device_id_type=MESH,
        ).start()

    last = KV_HEADS - 1

    def lay(code, blocks, blocks_last, slot):
        block = pool[jnp.clip(lax.rem(code, 128) - 1, 0, 63)]
        for c in range(last):
            blocks[c, slot, :, :HEAD_DIM] = block[:, c * HEAD_DIM : (c + 1) * HEAD_DIM]
            blocks[c, slot, :, HEAD_DIM:] = block[:, (8 + c) * HEAD_DIM : (9 + c) * HEAD_DIM]
        blocks_last[0, slot] = block[:, last * HEAD_DIM : KV_HEADS * HEAD_DIM]
        blocks_last[1, slot] = block[:, (8 + last) * HEAD_DIM :]

    def send_one(source, target, n, i):
        pltpu.make_async_remote_copy(
            source.at[i - 1],
            target.at[i - 1],
            send_sem.at[n],
            recv_sem.at[n],
            device_id=partner(i),
            device_id_type=MESH,
        ).start()

    second = pltpu.make_async_copy(
        asked.at[pl.ds(0, 120)], asked.at[pl.ds(8, 120)], ask_recv_sem.at[1]
    )
    second.wait()
    copy_all = pltpu.make_async_copy(asked, asked_all, ask_sem)
    copy_all.start()
    copy_all.wait()
    loads[1].wait()

    def stage_one(i, carry):
        lay(asked_all[gathered_row(*shifted(i)), 0, me], staged, staged_last, i - 1)
        return carry

    lax.fori_loop(1, N_ALL, stage_one, 0)

    def send(c):
        def one(i, carry):
            send_one(staged.at[c], arrived.at[c], c, i)
            return carry

        lax.fori_loop(1, N_ALL, one, 0)

    def send_last(n):
        def one(i, carry):
            send_one(staged_last.at[n], arrived_last.at[n], last + n, i)
            return carry

        lax.fori_loop(1, N_ALL, one, 0)

    for c in range(AHEAD):
        send(c)

    lay(asked_all[0, 0, me], arrived, arrived_last, 127)

    suffix = steps.shape[0]
    rows = lax.broadcasted_iota(jnp.int32, (suffix, suffix), 0)
    lower = rows >= lax.broadcasted_iota(jnp.int32, (suffix, suffix), 1)
    total = exact_dot(jnp.where(lower, 1.0, 0.0), steps[...] * decay[...], ((1,), (0,)))
    heads = total.shape[1]
    high, low = split(jnp.exp(-total))
    rise_pair[:, :heads] = high
    rise_pair[:, heads:] = low
    high, low = split(jnp.exp(total) * steps[...])
    fall_pair[:, :heads] = high
    fall_pair[:, heads:] = low
    high, low = split(jnp.broadcast_to(skip[...], (16, heads)))
    skip_pair[:, :heads] = high
    skip_pair[:, heads:] = low
    inter = jnp.where(lower, exact_dot(out_map[...], in_map[...], ((0,), (0,))), 0.0)
    high, low = split(inter)
    inter_high[...] = high
    inter_low[...] = low
    high, low = split(out_map[...])
    out_pair[...] = jnp.concatenate([high, low], axis=0)

    holder = lax.broadcasted_iota(jnp.int32, (N_ALL, N_ALL * BLK), 0)
    offset = lax.broadcasted_iota(jnp.int32, (N_ALL, N_ALL * BLK), 1) // BLK + 1
    a, b, c, e = shifted(offset % N_ALL)
    source = ((g + 4 - a) % 4) * 32 + ((y + 4 - b) % 4) * 8 + ((z + 4 - c) % 4) * 2 + (core + e) % 2
    chosen = jnp.where(holder == source, 1.0, 0.0).astype(BF16)
    live = jnp.where(wanted > 0.5, 1.0, 0.0).astype(BF16)
    seen = dot(jnp.broadcast_to(live, (16, N_ALL)), chosen)
    bias[...] = jnp.where(seen[:8] > 0.5, 0.0, -1e30)

    pltpu.make_async_copy(state_out, state_in.at[0:3], state_recv_sem).wait()
    loads[2].wait()
    which = lax.rem(g - state_group[0] + 7, 4)

    def mix(j, carry):
        columns = pl.ds(pl.multiple_of(j * MIX_BLOCK, MIX_BLOCK), MIX_BLOCK)
        row = lax.broadcasted_iota(jnp.int32, (2 * heads, MIX_BLOCK), 0) % heads
        head = (lax.broadcasted_iota(jnp.int32, (2 * heads, MIX_BLOCK), 1) + j * MIX_BLOCK) // SSM_HEAD_DIM
        spread = jnp.where(row == head, 1.0, 0.0).astype(BF16)
        values = inputs[:, columns].astype(F32)
        high, low = split(dot(fall_pair[...], spread) * values)
        start = state_in[which, :, columns]
        inner = dot(inter_high[...], high) + dot(inter_low[...], high) + dot(inter_high[...], low)
        inner = inner + dot(out_pair[...], jnp.concatenate([start, start], axis=0), ((0,), (0,)))
        result = dot(rise_pair[...], spread) * inner + dot(skip_pair[...], spread)[:1] * values
        mixed[:, columns] = result.astype(BF16)
        return carry

    lax.fori_loop(0, inputs.shape[1] // MIX_BLOCK, mix, 0)

    loads[3].wait()
    loads[4].wait()
    group = queries.shape[1] // (KV_HEADS * HEAD_DIM)
    scale = HEAD_DIM ** (-0.5)

    def wait_for(sem, n, source, target):
        slots = pl.ds(0, N_ALL - 1)
        pltpu.make_async_copy(source.at[slots], target.at[slots], sem.at[n]).wait()

    def columns_of(c, h):
        return pl.ds(pl.multiple_of((c * group + h) * HEAD_DIM, HEAD_DIM), HEAD_DIM)

    def own(c):
        return (
            new[:, pl.ds(pl.multiple_of(c * HEAD_DIM, HEAD_DIM), HEAD_DIM)],
            new[:, pl.ds(pl.multiple_of((c + 8) * HEAD_DIM, HEAD_DIM), HEAD_DIM)],
        )

    def softmax(query, keys, keys_new):
        old = dot(query, keys, ((1,), (1,))) * scale + bias[0:1]
        fresh = jnp.where(lower, dot(query, keys_new, ((1,), (1,))) * scale, -1e30)
        peak = jnp.maximum(
            jnp.max(old, axis=1, keepdims=True), jnp.max(fresh, axis=1, keepdims=True)
        )
        old = jnp.exp(old - peak)
        fresh = jnp.exp(fresh - peak)
        return old, fresh, jnp.sum(old, axis=1, keepdims=True) + jnp.sum(fresh, axis=1, keepdims=True)

    def attend(c, carry):
        wait_for(recv_sem, c, staged.at[c], arrived.at[c])
        keys = arrived[c, :, :, :HEAD_DIM].reshape(N_ALL * BLK, HEAD_DIM)
        values = arrived[c, :, :, HEAD_DIM:].reshape(N_ALL * BLK, HEAD_DIM)
        keys_new, values_new = own(c)

        def one(h, carry):
            old, fresh, weight = softmax(queries[:, columns_of(c, h)], keys, keys_new)
            result = dot(old.astype(BF16), values) + dot(fresh.astype(BF16), values_new)
            attended[:, columns_of(c, h)] = (result / weight).astype(BF16)
            return carry

        lax.fori_loop(0, group, one, 0)

        @pl.when(c + AHEAD < last)
        def _():
            send(c + AHEAD)

        @pl.when(c + AHEAD == last)
        def _():
            send_last(0)
            send_last(1)

        return carry

    lax.fori_loop(0, last, attend, 0)

    keys_new, values_new = own(last)
    wait_for(recv_sem, last, staged_last.at[0], arrived_last.at[0])
    keys = arrived_last[0].reshape(N_ALL * BLK, HEAD_DIM)

    def weigh(h, carry):
        old, fresh, weight = softmax(queries[:, columns_of(last, h)], keys, keys_new)
        weights[h] = jnp.broadcast_to(weight, (suffix, HEAD_DIM))
        partial[h] = dot(fresh.astype(BF16), values_new)
        rounded[h] = old.astype(BF16)
        return carry

    lax.fori_loop(0, group, weigh, 0)
    wait_for(recv_sem, last + 1, staged_last.at[1], arrived_last.at[1])
    values = arrived_last[1].reshape(N_ALL * BLK, HEAD_DIM)

    def finish(h, carry):
        result = dot(rounded[h], values) + partial[h]
        attended[:, columns_of(last, h)] = (result / weights[h]).astype(BF16)
        return carry

    lax.fori_loop(0, group, finish, 0)

    pltpu.make_async_copy(asked.at[pl.ds(0, 7)], asked.at[pl.ds(1, 7)], ask_send_sem.at[0]).wait()
    pltpu.make_async_copy(
        asked.at[pl.ds(0, 120)], asked.at[pl.ds(8, 120)], ask_send_sem.at[1]
    ).wait()
    pltpu.make_async_copy(state_out, state_in.at[0:3], state_send_sem).wait()
    for c in range(last):
        wait_for(send_sem, c, staged.at[c], arrived.at[c])
    for n in range(2):
        wait_for(send_sem, last + n, staged_last.at[n], arrived_last.at[n])


def body(
    queries,
    new_kv,
    kv_pool,
    hit_holder,
    hit_block,
    hit_count,
    ssm_input,
    step_size,
    decay_rate,
    state_in,
    state_out,
    skip_gain,
    state_pool,
    state_group,
    state_slot,
):
    n_all = lax.axis_size(("grp", "dev"))
    suffix, channels = ssm_input.shape
    heads = decay_rate.shape[0]
    group = queries.shape[1] // (KV_HEADS * HEAD_DIM)
    states = state_in.shape[1]
    smem = pl.BlockSpec(memory_space=pltpu.SMEM)
    vmem = pl.BlockSpec(memory_space=pltpu.VMEM)
    left = pl.BlockSpec(memory_space=pl.ANY)
    return pl.pallas_call(
        kernel,
        name="prefill",
        out_shape=(
            pltpu.VMEM(queries.shape, BF16),
            pltpu.VMEM(ssm_input.shape, BF16),
        ),
        in_specs=[smem] * 3 + [vmem] * 7 + [left] * 5,
        out_specs=(vmem, vmem),
        scratch_shapes=[
            pltpu.VMEM(kv_pool.shape, BF16),
            pltpu.VMEM(state_pool.shape, F32),
            pltpu.VMEM(queries.shape, BF16),
            pltpu.VMEM(new_kv.shape, BF16),
            pltpu.VMEM(ssm_input.shape, BF16),
            pltpu.VMEM((KV_HEADS - 1, n_all, BLK, 2 * HEAD_DIM), BF16),
            pltpu.VMEM((KV_HEADS - 1, n_all, BLK, 2 * HEAD_DIM), BF16),
            pltpu.VMEM((2, n_all, BLK, HEAD_DIM), BF16),
            pltpu.VMEM((2, n_all, BLK, HEAD_DIM), BF16),
            pltpu.VMEM((3, states, channels), BF16),
            pltpu.VMEM((4, states, channels), BF16),
            pltpu.VMEM((n_all, 1, n_all), jnp.int32),
            pltpu.SMEM((n_all, 1, n_all), jnp.int32),
            pltpu.VMEM((group, suffix, HEAD_DIM), F32),
            pltpu.VMEM((group, suffix, HEAD_DIM), F32),
            pltpu.VMEM((group, suffix, n_all * BLK), BF16),
            pltpu.VMEM((8, n_all * BLK), F32),
            pltpu.VMEM((suffix, 2 * heads), BF16),
            pltpu.VMEM((suffix, 2 * heads), BF16),
            pltpu.VMEM((16, 2 * heads), BF16),
            pltpu.VMEM((suffix, suffix), BF16),
            pltpu.VMEM((suffix, suffix), BF16),
            pltpu.VMEM((2 * states, suffix), BF16),
            pltpu.SemaphoreType.DMA((5,)),
            pltpu.SemaphoreType.DMA((KV_HEADS + 1,)),
            pltpu.SemaphoreType.DMA((KV_HEADS + 1,)),
            pltpu.SemaphoreType.DMA,
            pltpu.SemaphoreType.DMA,
            pltpu.SemaphoreType.DMA((2,)),
            pltpu.SemaphoreType.DMA((2,)),
            pltpu.SemaphoreType.DMA,
        ],
        compiler_params=pltpu.CompilerParams(
            collective_id=0, has_side_effects=True, vmem_limit_bytes=VMEM_LIMIT
        ),
    )(
        state_group,
        state_slot,
        hit_count,
        hit_holder,
        hit_block,
        step_size,
        decay_rate[None, :],
        state_in.T,
        state_out.T,
        skip_gain[None, :],
        queries,
        new_kv,
        kv_pool,
        ssm_input,
        state_pool,
    )


def solution(mesh):
    return jax.shard_map(
        body,
        mesh=mesh,
        in_specs=(
            P(("grp", "dev"), None),
            P(("grp", "dev"), None),
            P(("grp", "dev"), None, None),
            P(("grp", "dev"), None),
            P(("grp", "dev"), None),
            P(("grp", "dev")),
            P(("grp", "dev"), None),
            P(("grp", "dev"), None),
            P(),
            P(("grp", "dev"), None),
            P(("grp", "dev"), None),
            P(),
            P(("grp", "dev"), None, None),
            P(("grp", "dev")),
            P(("grp", "dev")),
        ),
        out_specs=(P(("grp", "dev"), None), P(("grp", "dev"), None)),
        check_vma=False,
    )
```
